32 devices in a mesh: groups: 2 (over y), row: 4 (over z), col: 4 (over x, core).
Axes of the slice: x: 2, y: 2, z: 4, core: 2. Of those that a mesh axis runs over, the one named last changes fastest.
Arguments:
- slip: float32 [32, 16, 243], P(('groups', 'row', 'col')), parts along dimension 0, may hold values from -6 to 6
- inverse: float32 [32, 486, 243], P(('groups', 'row', 'col')), parts along dimension 0, may hold values from -0.6 to 0.6
- positions: float32 [32, 3, 81], P('groups'), parts along dimension 0
Outputs:
- updated: float32 [32, 16, 243], P(('groups', 'row', 'col')), parts along dimension 0
- residual: float32 [32, 16, 243], P(('groups', 'row', 'col')), parts along dimension 0
The draws below stay inside these ranges and needn't reach their ends.
There are 2 independent parts, one for each index of `groups`. The reference program is written for one: setup_inputs(seed, part) draws one part's arguments, and reference() takes and returns one part's arrays. A program takes and returns all parts, laid end to end along the dimension named above; each array names one. Nothing has to cross between parts.
All inputs are finite; a program needn't handle non-finite values.
Results may differ from the reference program's by a relative error of at most 0.0041.
Values may be sent and summed in bfloat16 or wider, within the bound.
A program may use at most 64 MiB of HBM per device.

```python
import math
import jax
import jax.numpy as jnp
from jax import lax

BLOBS = 162
COLS = 16
HALF = 81
BLOCKS = 16
BODIES = 8


def draw_inverse(key, part):
    matrix_order = 3 * BLOBS
    narrow = 3 * HALF
    spread = 0.35 / math.sqrt(matrix_order)
    diagonal = jax.random.uniform(jax.random.fold_in(key, 12), (BLOCKS, narrow), jnp.float32, 0.2, 0.4)
    off_diag = jax.random.uniform(jax.random.fold_in(key, 11), (BLOCKS, matrix_order, narrow), jnp.float32, -spread, spread)
    row_ids = jnp.arange(matrix_order, dtype=jnp.int32)[None, :, None]
    col_ids = jnp.arange(narrow, dtype=jnp.int32)[None, None, :]
    half_ids = (jnp.arange(BLOCKS, dtype=jnp.int32) % 2)[:, None, None]
    on_diag = row_ids == half_ids * narrow + col_ids
    return off_diag + jnp.where(on_diag, diagonal[:, None, :], 0.0)


def draw_positions(key, part):
    lattice_side = int(math.ceil(BODIES ** (1.0 / 3.0)))
    if lattice_side ** 3 < BODIES:
        lattice_side = lattice_side + 1
    spacing = 8.0
    jitter = 1.0
    step_lo = 1.5
    step_hi = 2.5
    lattice_sites = jax.random.permutation(jax.random.fold_in(key, 21), lattice_side ** 3)[:BODIES]
    grid_coords = jnp.stack([lattice_sites // (lattice_side * lattice_side), lattice_sites // lattice_side % lattice_side, lattice_sites % lattice_side], axis=1).astype(jnp.float32)
    centers = grid_coords * spacing + jax.random.uniform(jax.random.fold_in(key, 22), (BODIES, 3), jnp.float32, -jitter, jitter)
    directions = jax.random.normal(jax.random.fold_in(key, 23), (BODIES, 3, BLOBS), jnp.float32)
    directions = directions / jnp.sqrt(jnp.sum(directions * directions, axis=1, keepdims=True) + 1e-06)
    step_length = jax.random.uniform(jax.random.fold_in(key, 24), (BODIES, 1, BLOBS), jnp.float32, step_lo, step_hi)
    path = jnp.cumsum(directions * step_length, axis=2)
    path = path - jnp.mean(path, axis=2, keepdims=True)
    placed = centers[:, :, None] + path
    return placed.reshape(BODIES, 3, 2, HALF).transpose(0, 2, 1, 3).reshape(BLOCKS, 3, HALF)


def block_scale(rng, dims, shards, low, high):
    def one(axis_at, parts):
        steps = jax.random.uniform(jax.random.fold_in(jax.random.fold_in(rng, 6), axis_at), (parts,), jnp.float32, low / len(shards), high / len(shards))
        return jnp.repeat(jnp.exp(steps), dims[axis_at] // parts).reshape((-1,) + (1,) * (len(dims) - axis_at - 1))

    loudness = one(*shards[0])
    for cut in shards[1:]:
        loudness = loudness * one(*cut)
    return loudness


def centred(rng, shape, scale, most, split=(), kind=jnp.bfloat16):
    factor_of = block_scale(rng, shape, split, -0.22, 0.18) if split else 1.0
    drawn = jax.random.normal(rng, shape, jnp.float32) * scale * factor_of
    return jnp.minimum(jnp.maximum(drawn, -most), most).astype(kind)


def setup_inputs(seed: int = 0, part: int = 0) -> dict:
    key_list = jax.random.split(jax.random.key(seed), 4)
    part_splits = jax.random.split(jax.random.fold_in(key_list[3], part), 4)
    return {
        "slip": centred(part_splits[0], (BLOCKS, COLS, 3 * HALF), 1.0, 6.0, ((0, 16),), jnp.float32),
        "inverse": draw_inverse(jax.random.fold_in(jax.random.fold_in(key_list[3], part), 71), part),
        "positions": draw_positions(jax.random.fold_in(jax.random.fold_in(key_list[3], part), 71), part),
    }


def rpy_tiles(left_pos, right_pos):
    separation = left_pos[:, :, :, None] - right_pos[:, :, None, :]
    dist_sq = lax.optimization_barrier(jnp.sum(separation * separation, axis=1))
    distance = jnp.sqrt(dist_sq)
    far_dist = jnp.maximum(distance, 2.0)
    near_safe = jnp.where(dist_sq > 0.0, distance, 1.0)
    far_mask = dist_sq >= 4.0
    isotropic = jnp.where(far_mask, 0.75 / far_dist * (1.0 + 2.0 / (3.0 * far_dist * far_dist)), 1.0 - 9.0 * distance / 32.0)
    anisotropic = jnp.where(far_mask, 0.75 / far_dist * (1.0 - 2.0 / (far_dist * far_dist)) / (far_dist * far_dist), 3.0 / (32.0 * near_safe))
    first_part = separation[:, :, :, None, :]
    second_part = jnp.swapaxes(separation, 1, 2)[:, None, :, :, :]
    tensor = anisotropic[:, None, :, None, :] * first_part * second_part
    identity_part = jnp.eye(3, dtype=jnp.float32)[None, :, None, :, None]
    tensor = tensor + identity_part * isotropic[:, None, :, None, :]
    tile_count = left_pos.shape[0]
    matrix_order = 3 * left_pos.shape[2]
    return tensor.reshape(tile_count, matrix_order, matrix_order).astype(jnp.bfloat16)

def join_halves(values):
    return values.reshape(BODIES, 2, COLS, 3 * HALF).transpose(0, 2, 1, 3).reshape(BODIES, COLS, 6 * HALF)

def reference(slip, inverse, positions):
    inverse_pairs = inverse.reshape(BODIES, 2, 6 * HALF, 3 * HALF)
    force = jnp.einsum('bsq,bhqp->bhsp', join_halves(slip), inverse_pairs, precision=lax.Precision.HIGHEST).reshape(BLOCKS, COLS, 3 * HALF)
    force_wire = lax.optimization_barrier(force.astype(jnp.bfloat16)).astype(jnp.float32)

    def one_row(row_index):
        left_pos = jnp.broadcast_to(positions[row_index][None], positions.shape)
        tile_blocks = rpy_tiles(left_pos, positions).astype(jnp.float32)
        return jnp.einsum('qsc,qrc->sr', force_wire, tile_blocks, precision=lax.Precision.HIGHEST)
    velocity = lax.map(one_row, jnp.arange(BLOCKS, dtype=jnp.int32))
    residual = slip - velocity
    correction = jnp.einsum('bsq,bhqp->bhsp', join_halves(residual), inverse_pairs, precision=lax.Precision.HIGHEST).reshape(BLOCKS, COLS, 3 * HALF)
    return (force + correction, residual)
```

```python
import functools

import jax
import jax.numpy as jnp
from jax import lax
from jax.experimental import pallas as pl
from jax.experimental.pallas import tpu as pltpu
from jax.sharding import PartitionSpec as P

MESH = pl.DeviceIdType.MESH
LANES = 128
CHUNK = 16


def round_up(value, step):
    return -(-value // step) * step


def split(value):
    high = value.astype(jnp.bfloat16)
    low = (value - high.astype(jnp.float32)).astype(jnp.bfloat16)
    return high, low


def triple(rows, blobs, wide):
    lane = lax.broadcasted_iota(jnp.int32, rows.shape, rows.ndim - 1)
    axis = rows.ndim - 1
    once = pltpu.roll(rows, blobs, axis)
    twice = pltpu.roll(rows, 2 * blobs, axis)
    return jnp.where(lane < blobs, rows, jnp.where(lane < 2 * blobs, once, twice))


def kernel(
    row_count, col_count, blobs,
    slip_ref, inverse_ref, positions_ref,
    updated_ref, residual_ref,
    inverse_buf, inv_high, inv_low, tiles, own, source, other_slip, other_res, forces,
    inverse_sem, slip_sems, res_sems, send_sems, recv_sems,
):
    count = row_count * col_count
    row = lax.axis_index("row")
    col = lax.axis_index("col")
    me = row * col_count + col
    half = col % 2
    partner = col + 1 - 2 * half
    narrow = 3 * blobs
    wide = source.shape[-1]
    pad = own.shape[1]

    load = pltpu.make_async_copy(inverse_ref.at[0], inverse_buf, inverse_sem)
    load.start()

    barrier = pltpu.get_barrier_semaphore()

    def place(step):
        there = lax.rem(me + step, count)
        return there, {"row": there // col_count, "col": lax.rem(there, col_count)}

    def greet(step, carry):
        pl.semaphore_signal(barrier, inc=1, device_id=place(step)[1], device_id_type=MESH)
        return carry

    lax.fori_loop(1, count, greet, 0)

    def prepare(q, carry):
        rows = jnp.pad(positions_ref[q], ((0, 5), (0, wide - blobs)))
        spread = triple(rows, blobs, wide)
        lane = lax.broadcasted_iota(jnp.int32, (1, wide), 1)
        mixed = jnp.where(
            lane < blobs, spread[0:1], jnp.where(lane < 2 * blobs, spread[1:2], spread[2:3])
        )
        source[q, 0:3, :] = spread[0:3]
        source[q, 3:4, :] = mixed
        return carry

    lax.fori_loop(0, count, prepare, 0)
    own_rows = jnp.pad(positions_ref[me], ((0, 5), (0, LANES - blobs)))
    own_cols = own_rows.T
    lane = lax.broadcasted_iota(jnp.int32, (pad, wide), 1)
    parts = [jnp.broadcast_to(own_cols[:pad, a : a + 1], (pad, wide)) for a in range(3)]
    for a in range(3):
        own[a] = parts[a]
    own[3] = jnp.where(lane < blobs, parts[0], jnp.where(lane < 2 * blobs, parts[1], parts[2]))

    def build(q, carry):
        lane = lax.broadcasted_iota(jnp.int32, (CHUNK, wide), 1)
        masks = [(lane >= a * blobs) & (lane < (a + 1) * blobs) for a in range(3)]
        there = [jnp.broadcast_to(source[q, a : a + 1, :], (CHUNK, wide)) for a in range(4)]
        for at in range(0, pad, CHUNK):
            d0, d1, d2, db = [own[a, at : at + CHUNK, :] - there[a] for a in range(4)]
            dist_sq = d0 * d0 + d1 * d1 + d2 * d2
            r = lax.rsqrt(jnp.where(dist_sq > 0.0, dist_sq, 1.0))
            r2 = r * r
            t = 0.75 * r
            u = t * r2
            far = dist_sq >= 4.0
            isotropic = jnp.where(far, t + (2.0 / 3.0) * u, 1.0 - (9.0 / 32.0) * (dist_sq * r))
            anisotropic = jnp.where(far, u - (2.0 * u) * r2, (3.0 / 32.0) * r)
            scaled = anisotropic * db
            for a, da in enumerate((d0, d1, d2)):
                value = scaled * da + jnp.where(masks[a], isotropic, 0.0)
                tiles[q, a * pad + at : a * pad + at + CHUNK, :] = value.astype(jnp.bfloat16)
        return carry

    lax.fori_loop(0, count // 2, build, 0)

    pl.semaphore_wait(barrier, count - 1)

    def swap(source_ref, target_ref, sems):
        return pltpu.make_async_remote_copy(
            src_ref=source_ref,
            dst_ref=target_ref,
            send_sem=sems.at[0],
            recv_sem=sems.at[1],
            device_id={"col": partner},
            device_id_type=MESH,
        )

    slip_swap = swap(slip_ref.at[0], other_slip, slip_sems)
    slip_swap.start()

    load.wait()
    inv_high[...] = jnp.zeros_like(inv_high)
    inv_low[...] = jnp.zeros_like(inv_low)
    for h in range(2):
        high, low = split(inverse_buf[h * narrow : (h + 1) * narrow, :])
        inv_high[h, :narrow, :narrow] = high
        inv_low[h, :narrow, :narrow] = low

    def apply(values, h):
        high, low = split(values)
        big = inv_high[h, :narrow, :]
        small = inv_low[h, :narrow, :]
        rows = values.shape[0]
        both = jnp.dot(
            jnp.concatenate([high, low], axis=0), big, preferred_element_type=jnp.float32
        )
        cross = jnp.dot(high, small, preferred_element_type=jnp.float32)
        return both[:rows] + (both[rows:] + cross)

    force = apply(slip_ref[0], half)
    slip_swap.wait()
    force = force + apply(other_slip[...], 1 - half)
    forces[me] = force.astype(jnp.bfloat16)

    def send(step):
        there, device = place(step)
        return pltpu.make_async_remote_copy(
            src_ref=forces.at[me],
            dst_ref=forces.at[me],
            send_sem=send_sems.at[step],
            recv_sem=recv_sems.at[me],
            device_id=device,
            device_id_type=MESH,
        )

    def start_send(step, carry):
        send(step).start()
        return carry

    lax.fori_loop(1, count, start_send, 0)

    lax.fori_loop(count // 2, count, build, 0)

    def receive(q):
        pltpu.make_async_remote_copy(
            src_ref=forces.at[q],
            dst_ref=forces.at[q],
            send_sem=send_sems.at[0],
            recv_sem=recv_sems.at[q],
            device_id={"col": partner},
            device_id_type=MESH,
        ).wait_recv()

    def product(q):
        return lax.dot_general(
            forces[q], tiles[q], (((1,), (1,)), ((), ())), preferred_element_type=jnp.float32
        )

    def gather(turn, total):
        for c in range(col_count):
            step = turn * col_count + c
            q = lax.rem(me + step, count)

            @pl.when(step > 0)
            def _():
                receive(q)

            total = total + product(q)
        return total

    rows = slip_ref.shape[1]
    total = lax.fori_loop(0, row_count, gather, jnp.zeros((rows, 3 * pad), jnp.float32))
    total = jnp.pad(total, ((0, 0), (0, round_up(3 * pad, LANES) - 3 * pad)))
    full = total.shape[1]
    lane = lax.broadcasted_iota(jnp.int32, total.shape, 1)
    shift = pad - blobs
    velocity = jnp.where(
        lane < blobs,
        total,
        jnp.where(
            lane < 2 * blobs,
            pltpu.roll(total, full - shift, 1),
            pltpu.roll(total, full - 2 * shift, 1),
        ),
    )
    residual = slip_ref[0] - velocity[:, :narrow]
    residual_ref[0] = residual
    res_swap = swap(residual_ref.at[0], other_res, res_sems)
    res_swap.start()
    updated = force + apply(residual, half)

    def end_send(step, carry):
        send(step).wait_send()
        return carry

    lax.fori_loop(1, count, end_send, 0)
    res_swap.wait()
    updated = updated + apply(other_res[...], 1 - half)
    updated_ref[0] = updated[:, :narrow]


def local(slip, inverse, positions):
    row_count = lax.axis_size("row")
    col_count = lax.axis_size("col")
    count = row_count * col_count
    blobs = positions.shape[2]
    rows, narrow = slip.shape[1:]
    wide = round_up(narrow, LANES)
    pad = round_up(blobs, CHUNK)
    vmem = pl.BlockSpec(memory_space=pltpu.VMEM)
    f32, bf16 = jnp.float32, jnp.bfloat16
    updated, residual = pl.pallas_call(
        functools.partial(kernel, row_count, col_count, blobs),
        out_shape=(
            jax.ShapeDtypeStruct(slip.shape, f32),
            jax.ShapeDtypeStruct(slip.shape, f32),
        ),
        in_specs=[vmem, pl.BlockSpec(memory_space=pl.ANY), vmem],
        out_specs=(vmem, vmem),
        scratch_shapes=[
            pltpu.VMEM(inverse.shape[1:], f32),
            pltpu.VMEM((2, round_up(narrow, CHUNK), wide), bf16),
            pltpu.VMEM((2, round_up(narrow, CHUNK), wide), bf16),
            pltpu.VMEM((count, 3 * pad, wide), bf16),
            pltpu.VMEM((4, pad, wide), f32),
            pltpu.VMEM((count, 8, wide), f32),
            pltpu.VMEM((rows, narrow), f32),
            pltpu.VMEM((rows, narrow), f32),
            pltpu.VMEM((count, rows, wide), bf16),
            pltpu.SemaphoreType.DMA,
            pltpu.SemaphoreType.DMA((2,)),
            pltpu.SemaphoreType.DMA((2,)),
            pltpu.SemaphoreType.DMA((count,)),
            pltpu.SemaphoreType.DMA((count,)),
        ],
        compiler_params=pltpu.CompilerParams(
            collective_id=0, has_side_effects=True, vmem_limit_bytes=60 * 1024 * 1024
        ),
    )(slip, inverse, positions)
    return updated, residual


def solution(mesh):
    in_specs = (
        P(("groups", "row", "col"), None, None),
        P(("groups", "row", "col"), None, None),
        P("groups", None, None),
    )
    out_specs = (P(("groups", "row", "col"), None, None), P(("groups", "row", "col"), None, None))
    return jax.shard_map(local, mesh=mesh, in_specs=in_specs, out_specs=out_specs, check_vma=False)
```

```python
import functools

import jax
import jax.numpy as jnp
from jax import lax
from jax.experimental import pallas as pl
from jax.experimental.pallas import tpu as pltpu
from jax.sharding import PartitionSpec as P

MESH = pl.DeviceIdType.MESH
LANES = 128
CHUNK = 16


def round_up(value, step):
    return -(-value // step) * step


def split(value):
    high = value.astype(jnp.bfloat16)
    low = (value - high.astype(jnp.float32)).astype(jnp.bfloat16)
    return high, low


def triple(rows, blobs):
    lane = lax.broadcasted_iota(jnp.int32, rows.shape, rows.ndim - 1)
    axis = rows.ndim - 1
    once = pltpu.roll(rows, blobs, axis)
    twice = pltpu.roll(rows, 2 * blobs, axis)
    return jnp.where(lane < blobs, rows, jnp.where(lane < 2 * blobs, once, twice))


def kernel(
    row_count, col_count, blobs,
    slip_hbm, inverse_hbm, positions_hbm,
    updated, residual,
    slip, inverse, positions,
    inv_high, inv_low, tiles, own_rows, own, source, other_slip, part, other_part, forces, held,
    load_sems, slip_sems, part_sems, send_sems, recv_sems,
):
    bodies = row_count * col_count // 2
    row = lax.axis_index("row")
    col = lax.axis_index("col")
    half = lax.rem(col, 2)
    partner = col + 1 - 2 * half
    body = (row * col_count + col) // 2
    narrow = 3 * blobs
    wide = source.shape[-1]
    pad = own.shape[2]

    barrier = pltpu.get_barrier_semaphore()

    def place(step):
        there = 2 * lax.rem(body + step, bodies) + half
        return {"row": there // col_count, "col": lax.rem(there, col_count)}

    def greet(step, carry):
        pl.semaphore_signal(barrier, inc=1, device_id=place(step), device_id_type=MESH)
        return carry

    pl.semaphore_signal(barrier, inc=1, device_id={"col": partner}, device_id_type=MESH)
    lax.fori_loop(1, bodies, greet, 0)

    loads = [
        pltpu.make_async_copy(positions_hbm, positions, load_sems.at[0]),
        pltpu.make_async_copy(slip_hbm.at[0], slip, load_sems.at[1]),
        pltpu.make_async_copy(inverse_hbm.at[:, 0, :], inverse, load_sems.at[2]),
    ]
    for load in loads:
        load.start()
    inv_high[...] = jnp.zeros_like(inv_high)
    inv_low[...] = jnp.zeros_like(inv_low)
    own_rows[...] = jnp.zeros_like(own_rows)
    loads[0].wait()

    lane = lax.broadcasted_iota(jnp.int32, source.shape[1:], 1)
    spread = []
    for a in range(3):
        rows = jnp.pad(positions[a], ((0, 0), (0, wide - blobs)))
        spread.append(triple(rows, blobs))
        source[a] = spread[a]
        for t in range(2):
            own_rows[3 * t + a : 3 * t + a + 1, :blobs] = positions[a, pl.ds(2 * body + t, 1), :]
    source[3] = jnp.where(
        lane < blobs, spread[0], jnp.where(lane < 2 * blobs, spread[1], spread[2])
    )
    own_cols = own_rows[...].T
    lane = lax.broadcasted_iota(jnp.int32, (pad, wide), 1)
    for t in range(2):
        cols = [
            jnp.broadcast_to(own_cols[:pad, 3 * t + a : 3 * t + a + 1], (pad, wide))
            for a in range(3)
        ]
        for a in range(3):
            own[t, a] = cols[a]
        own[t, 3] = jnp.where(lane < blobs, cols[0], jnp.where(lane < 2 * blobs, cols[1], cols[2]))

    def build(step, carry):
        j = step // 2
        t = lax.rem(step, 2)
        lane = lax.broadcasted_iota(jnp.int32, (CHUNK, wide), 1)
        masks = [(lane >= a * blobs) & (lane < (a + 1) * blobs) for a in range(3)]
        there = [
            jnp.broadcast_to(source[a, pl.ds(2 * j + half, 1), :], (CHUNK, wide)) for a in range(4)
        ]
        for at in range(0, pad, CHUNK):
            d0, d1, d2, db = [own[t, a, at : at + CHUNK, :] - there[a] for a in range(4)]
            dist_sq = d0 * d0 + d1 * d1 + d2 * d2
            r = lax.rsqrt(jnp.where(dist_sq > 0.0, dist_sq, 1.0))
            r2 = r * r
            k = 0.75 * r
            u = k * r2
            far = dist_sq >= 4.0
            isotropic = jnp.where(far, k + (2.0 / 3.0) * u, 1.0 - (9.0 / 32.0) * (dist_sq * r))
            anisotropic = jnp.where(far, u - (2.0 * u) * r2, (3.0 / 32.0) * r)
            scaled = anisotropic * db
            for a, da in enumerate((d0, d1, d2)):
                value = scaled * da + jnp.where(masks[a], isotropic, 0.0)
                tiles[j, t, a * pad + at : a * pad + at + CHUNK, :] = value.astype(jnp.bfloat16)
        return carry

    first = bodies
    lax.fori_loop(0, first, build, 0)
    loads[1].wait()
    pl.semaphore_wait(barrier, bodies)

    def swap(source_ref, target_ref, sems):
        return pltpu.make_async_remote_copy(
            src_ref=source_ref,
            dst_ref=target_ref,
            send_sem=sems.at[0],
            recv_sem=sems.at[1],
            device_id={"col": partner},
            device_id_type=MESH,
        )

    slip_swap = swap(slip, other_slip, slip_sems)
    slip_swap.start()

    loads[2].wait()
    for h in range(2):
        high, low = split(inverse[h * narrow : (h + 1) * narrow, :])
        inv_high[h, :narrow, :narrow] = high
        inv_low[h, :narrow, :narrow] = low

    def apply(values, h):
        high, low = split(jnp.pad(values, ((0, 0), (0, wide - narrow))))
        big = inv_high[h]
        small = inv_low[h]
        rows = values.shape[0]
        both = jnp.dot(
            jnp.concatenate([high, low], axis=0), big, preferred_element_type=jnp.float32
        )
        cross = jnp.dot(high, small, preferred_element_type=jnp.float32)
        return both[:rows] + (both[rows:] + cross)

    force = apply(slip[...], half)
    slip_swap.wait()
    force = force + apply(other_slip[...], 1 - half)
    forces[body] = force.astype(jnp.bfloat16)
    held[...] = force

    def send(step):
        return pltpu.make_async_remote_copy(
            src_ref=forces.at[body],
            dst_ref=forces.at[body],
            send_sem=send_sems.at[step],
            recv_sem=recv_sems.at[body],
            device_id=place(step),
            device_id_type=MESH,
        )

    def start_send(step, carry):
        send(step).start()
        return carry

    lax.fori_loop(1, bodies, start_send, 0)

    lax.fori_loop(first, 2 * bodies, build, 0)

    def product(j):
        return lax.dot_general(
            forces[j],
            tiles[j].reshape(6 * pad, wide),
            (((1,), (1,)), ((), ())),
            preferred_element_type=jnp.float32,
        )

    def gather(step, total):
        j = lax.rem(body + step, bodies)
        pltpu.make_async_remote_copy(
            src_ref=forces.at[j],
            dst_ref=forces.at[j],
            send_sem=send_sems.at[0],
            recv_sem=recv_sems.at[j],
            device_id={"col": partner},
            device_id_type=MESH,
        ).wait_recv()
        return total + product(j)

    total = product(body)
    if bodies <= 8:
        for step in range(1, bodies):
            total = gather(step, total)
    else:
        total = lax.fori_loop(1, bodies, gather, total)
    full = round_up(6 * pad, LANES)
    total = jnp.pad(total, ((0, 0), (0, full - 6 * pad)))
    lane = lax.broadcasted_iota(jnp.int32, total.shape, 1)

    def moved(by):
        return pltpu.roll(total, full - by, 1) if by else total

    for t in range(2):
        start = 3 * t * pad
        shift = pad - blobs
        value = jnp.where(
            lane < blobs,
            moved(start),
            jnp.where(lane < 2 * blobs, moved(start + shift), moved(start + 2 * shift)),
        )
        part[t] = value[:, :wide]
    part_swap = swap(part, other_part, part_sems)
    part_swap.start()

    def end_send(step, carry):
        send(step).wait_send()
        return carry

    lax.fori_loop(1, bodies, end_send, 0)
    part_swap.wait()
    mine = slip[...] - (part[half] + other_part[half])[:, :narrow]
    residual[0] = mine
    theirs = other_slip[...] - (part[1 - half] + other_part[1 - half])[:, :narrow]
    result = held[...] + (apply(mine, half) + apply(theirs, 1 - half))
    updated[0] = result[:, :narrow]


def finish(updated, residual, updated_out, residual_out, sems):
    copies = [
        pltpu.make_async_copy(updated, updated_out, sems.at[0]),
        pltpu.make_async_copy(residual, residual_out, sems.at[1]),
    ]
    for copy in copies:
        copy.start()
    for copy in copies:
        copy.wait()


def stay(value):
    return pltpu.with_memory_space_constraint(value, pltpu.HBM)


def local(slip, inverse, positions):
    row_count = lax.axis_size("row")
    col_count = lax.axis_size("col")
    count = row_count * col_count
    bodies = count // 2
    blobs = positions.shape[2]
    rows, narrow = slip.shape[1:]
    wide = round_up(narrow, LANES)
    pad = round_up(blobs, CHUNK)
    vmem = pl.BlockSpec(memory_space=pltpu.VMEM)
    f32, bf16 = jnp.float32, jnp.bfloat16
    dma = pltpu.SemaphoreType.DMA
    tile_bytes = bodies * 6 * pad * wide * 2
    updated, residual = pl.pallas_call(
        functools.partial(kernel, row_count, col_count, blobs),
        out_shape=(
            pltpu.VMEM(slip.shape, f32),
            pltpu.VMEM(slip.shape, f32),
        ),
        in_specs=[pl.BlockSpec(memory_space=pltpu.HBM)] * 3,
        out_specs=(vmem, vmem),
        scratch_shapes=[
            pltpu.VMEM((rows, narrow), f32),
            pltpu.VMEM(inverse.shape[1:], f32),
            pltpu.VMEM((3, count, blobs), f32),
            pltpu.VMEM((2, wide, wide), bf16),
            pltpu.VMEM((2, wide, wide), bf16),
            pltpu.VMEM((bodies, 2, 3 * pad, wide), bf16),
            pltpu.VMEM((8, LANES), f32),
            pltpu.VMEM((2, 4, pad, wide), f32),
            pltpu.VMEM((4, count, wide), f32),
            pltpu.VMEM((rows, narrow), f32),
            pltpu.VMEM((2, rows, wide), f32),
            pltpu.VMEM((2, rows, wide), f32),
            pltpu.VMEM((bodies, rows, wide), bf16),
            pltpu.VMEM((rows, wide), f32),
            dma((3,)),
            dma((2,)),
            dma((2,)),
            dma((bodies,)),
            dma((bodies,)),
        ],
        compiler_params=pltpu.CompilerParams(
            collective_id=0,
            has_side_effects=True,
            vmem_limit_bytes=2 * tile_bytes if 2 * tile_bytes < 2**24 else 60 * 2**20,
        ),
    )(*(stay(v) for v in (slip, jnp.swapaxes(inverse, 0, 1), jnp.swapaxes(positions, 0, 1))))
    return pl.pallas_call(
        finish,
        out_shape=(jax.ShapeDtypeStruct(slip.shape, f32),) * 2,
        in_specs=[vmem, vmem],
        out_specs=(pl.BlockSpec(memory_space=pltpu.HBM),) * 2,
        scratch_shapes=[dma((2,))],
        compiler_params=pltpu.CompilerParams(vmem_limit_bytes=2**20),
    )(updated, residual)


def solution(mesh):
    in_specs = (
        P(("groups", "row", "col"), None, None),
        P(("groups", "row", "col"), None, None),
        P("groups", None, None),
    )
    out_specs = (P(("groups", "row", "col"), None, None), P(("groups", "row", "col"), None, None))
    return jax.shard_map(local, mesh=mesh, in_specs=in_specs, out_specs=out_specs, check_vma=False)
```

```python
import functools
import math

import jax
import jax.numpy as jnp
from jax import lax
from jax.experimental import pallas as pl
from jax.experimental.pallas import tpu as pltpu
from jax.sharding import PartitionSpec as P

MESH = pl.DeviceIdType.MESH
LANES = 128
CHUNK = 16
GROUP = 2


def round_up(value, step):
    return -(-value // step) * step


def split(value):
    high = value.astype(jnp.bfloat16)
    low = (value - high.astype(jnp.float32)).astype(jnp.bfloat16)
    return high, low


def triple(rows, blobs):
    lane = lax.broadcasted_iota(jnp.int32, rows.shape, rows.ndim - 1)
    axis = rows.ndim - 1
    once = pltpu.roll(rows, blobs, axis)
    twice = pltpu.roll(rows, 2 * blobs, axis)
    return jnp.where(lane < blobs, rows, jnp.where(lane < 2 * blobs, once, twice))


def kernel(
    row_count, col_count, blobs,
    slip_hbm, inverse_hbm, positions_hbm,
    updated, residual,
    slip, inverse, positions,
    inv_high, inv_low, tiles, own_rows, own, source, other_slip, part, other_part, forces, held,
    load_sems, slip_sems, part_sems, send_sems, recv_sems,
):
    bodies = row_count * col_count // 2
    row = lax.axis_index("row")
    col = lax.axis_index("col")
    half = lax.rem(col, 2)
    partner = col + 1 - 2 * half
    body = (row * col_count + col) // 2
    narrow = 3 * blobs
    wide = source.shape[-1]
    pad = own.shape[2]

    barrier = pltpu.get_barrier_semaphore()

    low_side = row < row_count // 2

    def far(step):
        return jnp.where(low_side, bodies - 1 - step, step)

    def place(j):
        there = 2 * j + half
        return {"row": there // col_count, "col": lax.rem(there, col_count)}

    def each(action):
        def visit(step, carry):
            j = far(step)

            @pl.when(j != body)
            def _():
                action(j)

            return carry

        lax.fori_loop(0, bodies, visit, 0)

    def greet(j):
        pl.semaphore_signal(barrier, inc=1, device_id=place(j), device_id_type=MESH)

    each(greet)
    pl.semaphore_signal(barrier, inc=1, device_id={"col": partner}, device_id_type=MESH)

    loads = [
        pltpu.make_async_copy(positions_hbm, positions, load_sems.at[0]),
        pltpu.make_async_copy(slip_hbm.at[0], slip, load_sems.at[1]),
        pltpu.make_async_copy(inverse_hbm.at[:, 0, :], inverse, load_sems.at[2]),
    ]
    for load in loads:
        load.start()
    inv_high[...] = jnp.zeros_like(inv_high)
    inv_low[...] = jnp.zeros_like(inv_low)
    own_rows[...] = jnp.zeros_like(own_rows)
    loads[0].wait()

    lane = lax.broadcasted_iota(jnp.int32, source.shape[1:], 1)
    spread = []
    for a in range(3):
        rows = jnp.pad(positions[a], ((0, 0), (0, wide - blobs)))
        spread.append(triple(rows, blobs))
        source[a] = spread[a]
        for t in range(2):
            own_rows[3 * t + a : 3 * t + a + 1, :blobs] = positions[a, pl.ds(2 * body + t, 1), :]
    source[3] = jnp.where(
        lane < blobs, spread[0], jnp.where(lane < 2 * blobs, spread[1], spread[2])
    )
    own_cols = own_rows[...].T
    lane = lax.broadcasted_iota(jnp.int32, (pad, wide), 1)
    for t in range(2):
        cols = [
            jnp.broadcast_to(own_cols[:pad, 3 * t + a : 3 * t + a + 1], (pad, wide))
            for a in range(3)
        ]
        for a in range(3):
            own[t, a] = cols[a]
        own[t, 3] = jnp.where(lane < blobs, cols[0], jnp.where(lane < 2 * blobs, cols[1], cols[2]))

    def build(step, carry):
        j = step // 2
        t = lax.rem(step, 2)
        lane = lax.broadcasted_iota(jnp.int32, (CHUNK, wide), 1)
        masks = [(lane >= a * blobs) & (lane < (a + 1) * blobs) for a in range(3)]
        there = [
            jnp.broadcast_to(source[a, pl.ds(2 * j + half, 1), :], (CHUNK, wide)) for a in range(4)
        ]
        for at in range(0, pad, CHUNK):
            d0, d1, d2, db = [own[t, a, at : at + CHUNK, :] - there[a] for a in range(4)]
            dist_sq = d0 * d0 + d1 * d1 + d2 * d2
            r = lax.rsqrt(jnp.where(dist_sq > 0.0, dist_sq, 1.0))
            r2 = r * r
            k = 0.75 * r
            u = k * r2
            far = dist_sq >= 4.0
            isotropic = jnp.where(far, k + (2.0 / 3.0) * u, 1.0 - (9.0 / 32.0) * (dist_sq * r))
            anisotropic = jnp.where(far, u - (2.0 * u) * r2, (3.0 / 32.0) * r)
            scaled = anisotropic * db
            for a, da in enumerate((d0, d1, d2)):
                value = scaled * da + jnp.where(masks[a], isotropic, 0.0)
                tiles[j, t, a * pad + at : a * pad + at + CHUNK, :] = value.astype(jnp.bfloat16)
        return carry

    first = 0
    lax.fori_loop(0, first, build, 0)
    loads[1].wait()
    pl.semaphore_wait(barrier, bodies)

    def swap(source_ref, target_ref, sems):
        return pltpu.make_async_remote_copy(
            src_ref=source_ref,
            dst_ref=target_ref,
            send_sem=sems.at[0],
            recv_sem=sems.at[1],
            device_id={"col": partner},
            device_id_type=MESH,
        )

    slip_swap = swap(slip, other_slip, slip_sems)
    slip_swap.start()

    loads[2].wait()
    for h in range(2):
        high, low = split(inverse[h * narrow : (h + 1) * narrow, :])
        inv_high[h, :narrow, :narrow] = high
        inv_low[h, :narrow, :narrow] = low

    def apply(values, h):
        high, low = split(jnp.pad(values, ((0, 0), (0, wide - narrow))))
        big = inv_high[h]
        small = inv_low[h]
        rows = values.shape[0]
        both = jnp.dot(
            jnp.concatenate([high, low], axis=0), big, preferred_element_type=jnp.float32
        )
        cross = jnp.dot(high, small, preferred_element_type=jnp.float32)
        return both[:rows] + (both[rows:] + cross)

    force = apply(slip[...], half)
    slip_swap.wait()
    force = force + apply(other_slip[...], 1 - half)
    forces[body] = force.astype(jnp.bfloat16)
    held[...] = force

    def send(j):
        return pltpu.make_async_remote_copy(
            src_ref=forces.at[body],
            dst_ref=forces.at[body],
            send_sem=send_sems.at[j],
            recv_sem=recv_sems.at[body],
            device_id=place(j),
            device_id_type=MESH,
        )

    each(lambda j: send(j).start())

    lax.fori_loop(first, 2 * bodies, build, 0)

    def product(j):
        return lax.dot_general(
            forces[j],
            tiles[j].reshape(6 * pad, wide),
            (((1,), (1,)), ((), ())),
            preferred_element_type=jnp.float32,
        )

    def receive(j):
        @pl.when(j != body)
        def _():
            pltpu.make_async_remote_copy(
                src_ref=forces.at[j],
                dst_ref=forces.at[j],
                send_sem=send_sems.at[0],
                recv_sem=recv_sems.at[j],
                device_id={"col": partner},
                device_id_type=MESH,
            ).wait_recv()

    group = math.gcd(bodies, GROUP)

    def gather(turn, total):
        picks = [far(bodies - 1 - (turn * group + k)) for k in range(group)]
        for j in picks:
            receive(j)
        for j in picks:
            total = total + product(j)
        return total

    total = jnp.zeros((slip.shape[0], 6 * pad), jnp.float32)
    if bodies <= 8:
        for turn in range(bodies // group):
            total = gather(turn, total)
    else:
        total = lax.fori_loop(0, bodies // group, gather, total)
    full = round_up(6 * pad, LANES)
    total = jnp.pad(total, ((0, 0), (0, full - 6 * pad)))
    lane = lax.broadcasted_iota(jnp.int32, total.shape, 1)

    def moved(by):
        return pltpu.roll(total, full - by, 1) if by else total

    for t in range(2):
        start = 3 * t * pad
        shift = pad - blobs
        value = jnp.where(
            lane < blobs,
            moved(start),
            jnp.where(lane < 2 * blobs, moved(start + shift), moved(start + 2 * shift)),
        )
        part[t] = value[:, :wide]
    part_swap = swap(part, other_part, part_sems)
    part_swap.start()

    each(lambda j: send(j).wait_send())
    part_swap.wait()
    mine = slip[...] - (part[half] + other_part[half])[:, :narrow]
    residual[0] = mine
    theirs = other_slip[...] - (part[1 - half] + other_part[1 - half])[:, :narrow]
    result = held[...] + (apply(mine, half) + apply(theirs, 1 - half))
    updated[0] = result[:, :narrow]


def finish(updated, residual, updated_out, residual_out, sems):
    copies = [
        pltpu.make_async_copy(updated, updated_out, sems.at[0]),
        pltpu.make_async_copy(residual, residual_out, sems.at[1]),
    ]
    for copy in copies:
        copy.start()
    for copy in copies:
        copy.wait()


def stay(value):
    return pltpu.with_memory_space_constraint(value, pltpu.HBM)


def local(slip, inverse, positions):
    row_count = lax.axis_size("row")
    col_count = lax.axis_size("col")
    count = row_count * col_count
    bodies = count // 2
    blobs = positions.shape[2]
    rows, narrow = slip.shape[1:]
    wide = round_up(narrow, LANES)
    pad = round_up(blobs, CHUNK)
    vmem = pl.BlockSpec(memory_space=pltpu.VMEM)
    f32, bf16 = jnp.float32, jnp.bfloat16
    dma = pltpu.SemaphoreType.DMA
    tile_bytes = bodies * 6 * pad * wide * 2
    updated, residual = pl.pallas_call(
        functools.partial(kernel, row_count, col_count, blobs),
        out_shape=(
            pltpu.VMEM(slip.shape, f32),
            pltpu.VMEM(slip.shape, f32),
        ),
        in_specs=[pl.BlockSpec(memory_space=pltpu.HBM)] * 3,
        out_specs=(vmem, vmem),
        scratch_shapes=[
            pltpu.VMEM((rows, narrow), f32),
            pltpu.VMEM(inverse.shape[1:], f32),
            pltpu.VMEM((3, count, blobs), f32),
            pltpu.VMEM((2, wide, wide), bf16),
            pltpu.VMEM((2, wide, wide), bf16),
            pltpu.VMEM((bodies, 2, 3 * pad, wide), bf16),
            pltpu.VMEM((8, LANES), f32),
            pltpu.VMEM((2, 4, pad, wide), f32),
            pltpu.VMEM((4, count, wide), f32),
            pltpu.VMEM((rows, narrow), f32),
            pltpu.VMEM((2, rows, wide), f32),
            pltpu.VMEM((2, rows, wide), f32),
            pltpu.VMEM((bodies, rows, wide), bf16),
            pltpu.VMEM((rows, wide), f32),
            dma((3,)),
            dma((2,)),
            dma((2,)),
            dma((bodies,)),
            dma((bodies,)),
        ],
        compiler_params=pltpu.CompilerParams(
            collective_id=0,
            has_side_effects=True,
            vmem_limit_bytes=2 * tile_bytes if 2 * tile_bytes < 2**24 else 60 * 2**20,
        ),
    )(*(stay(v) for v in (slip, jnp.swapaxes(inverse, 0, 1), jnp.swapaxes(positions, 0, 1))))
    return pl.pallas_call(
        finish,
        out_shape=(jax.ShapeDtypeStruct(slip.shape, f32),) * 2,
        in_specs=[vmem, vmem],
        out_specs=(pl.BlockSpec(memory_space=pltpu.HBM),) * 2,
        scratch_shapes=[dma((2,))],
        compiler_params=pltpu.CompilerParams(vmem_limit_bytes=2**20),
    )(updated, residual)


def solution(mesh):
    in_specs = (
        P(("groups", "row", "col"), None, None),
        P(("groups", "row", "col"), None, None),
        P("groups", None, None),
    )
    out_specs = (P(("groups", "row", "col"), None, None), P(("groups", "row", "col"), None, None))
    return jax.shard_map(local, mesh=mesh, in_specs=in_specs, out_specs=out_specs, check_vma=False)
```

```python
import functools
import math

import jax
import jax.numpy as jnp
from jax import lax
from jax.experimental import pallas as pl
from jax.experimental.pallas import tpu as pltpu
from jax.sharding import PartitionSpec as P

MESH = pl.DeviceIdType.MESH
LANES = 128
CHUNK = 16
GROUP = 2


def round_up(value, step):
    return -(-value // step) * step


def split(value):
    high = value.astype(jnp.bfloat16)
    low = (value - high.astype(jnp.float32)).astype(jnp.bfloat16)
    return high, low


def triple(rows, blobs):
    lane = lax.broadcasted_iota(jnp.int32, rows.shape, rows.ndim - 1)
    axis = rows.ndim - 1
    once = pltpu.roll(rows, blobs, axis)
    twice = pltpu.roll(rows, 2 * blobs, axis)
    return jnp.where(lane < blobs, rows, jnp.where(lane < 2 * blobs, once, twice))


def kernel(
    row_count, col_count, blobs,
    slip_hbm, inverse_hbm, positions_hbm,
    updated, residual,
    slip, inverse, positions,
    inv_high, inv_low, tiles, own_rows, own, source, other_slip, part, other_part, forces, held,
    load_sems, slip_sems, part_sems, send_sems, recv_sems, go_sem,
):
    bodies = row_count * col_count // 2
    row = lax.axis_index("row")
    col = lax.axis_index("col")
    half = lax.rem(col, 2)
    partner = col + 1 - 2 * half
    body = (row * col_count + col) // 2
    narrow = 3 * blobs
    wide = source.shape[-1]
    pad = own.shape[2]

    barrier = pltpu.get_barrier_semaphore()

    low_side = row < row_count // 2

    def far(step):
        return jnp.where(low_side, bodies - 1 - step, step)

    def place(j):
        there = 2 * j + half
        return {"row": there // col_count, "col": lax.rem(there, col_count)}

    def each(action):
        def visit(step, carry):
            j = far(step)

            @pl.when(j != body)
            def _():
                action(j)

            return carry

        lax.fori_loop(0, bodies, visit, 0)

    def welcome(j):
        there = 2 * j
        device = {"row": there // col_count, "col": lax.rem(there, col_count)}
        pl.semaphore_signal(barrier, inc=1, device_id=device, device_id_type=MESH)

    each(welcome)

    @pl.when(half == 0)
    def _():
        pl.semaphore_signal(barrier, inc=1, device_id={"col": partner}, device_id_type=MESH)


    loads = [
        pltpu.make_async_copy(positions_hbm, positions, load_sems.at[0]),
        pltpu.make_async_copy(slip_hbm.at[0], slip, load_sems.at[1]),
        pltpu.make_async_copy(inverse_hbm.at[:, 0, :], inverse, load_sems.at[2]),
    ]
    for load in loads:
        load.start()
    inv_high[...] = jnp.zeros_like(inv_high)
    inv_low[...] = jnp.zeros_like(inv_low)
    own_rows[...] = jnp.zeros_like(own_rows)

    def build(step, carry):
        j = step // 2
        t = lax.rem(step, 2)
        lane = lax.broadcasted_iota(jnp.int32, (CHUNK, wide), 1)
        masks = [(lane >= a * blobs) & (lane < (a + 1) * blobs) for a in range(3)]
        there = [
            jnp.broadcast_to(source[a, pl.ds(2 * j + half, 1), :], (CHUNK, wide)) for a in range(4)
        ]
        for at in range(0, pad, CHUNK):
            d0, d1, d2, db = [own[t, a, at : at + CHUNK, :] - there[a] for a in range(4)]
            dist_sq = d0 * d0 + d1 * d1 + d2 * d2
            r = lax.rsqrt(jnp.where(dist_sq > 0.0, dist_sq, 1.0))
            r2 = r * r
            k = 0.75 * r
            u = k * r2
            far = dist_sq >= 4.0
            isotropic = jnp.where(far, k + (2.0 / 3.0) * u, 1.0 - (9.0 / 32.0) * (dist_sq * r))
            anisotropic = jnp.where(far, u - (2.0 * u) * r2, (3.0 / 32.0) * r)
            scaled = anisotropic * db
            for a, da in enumerate((d0, d1, d2)):
                value = scaled * da + jnp.where(masks[a], isotropic, 0.0)
                tiles[j, t, a * pad + at : a * pad + at + CHUNK, :] = value.astype(jnp.bfloat16)
        return carry

    loads[1].wait()

    def swap(source_ref, target_ref, sems):
        return pltpu.make_async_remote_copy(
            src_ref=source_ref,
            dst_ref=target_ref,
            send_sem=sems.at[0],
            recv_sem=sems.at[1],
            device_id={"col": partner},
            device_id_type=MESH,
        )

    slip_swap = swap(slip, other_slip, slip_sems)

    @pl.when(half == 1)
    def _():
        pl.semaphore_wait(barrier, 1)
        slip_swap.start()

    @pl.when(half == 0)
    def _():
        slip_swap.wait_recv()
        slip_swap.start()

    loads[2].wait()
    for h in range(2):
        high, low = split(inverse[h * narrow : (h + 1) * narrow, :])
        inv_high[h, :narrow, :narrow] = high
        inv_low[h, :narrow, :narrow] = low

    def apply(values, h):
        high, low = split(jnp.pad(values, ((0, 0), (0, wide - narrow))))
        big = inv_high[h]
        small = inv_low[h]
        rows = values.shape[0]
        both = jnp.dot(
            jnp.concatenate([high, low], axis=0), big, preferred_element_type=jnp.float32
        )
        cross = jnp.dot(high, small, preferred_element_type=jnp.float32)
        return both[:rows] + (both[rows:] + cross)

    force = apply(slip[...], half)
    slip_swap.wait_send()

    @pl.when(half == 1)
    def _():
        slip_swap.wait_recv()

    force = force + apply(other_slip[...], 1 - half)
    forces[body] = force.astype(jnp.bfloat16)
    held[...] = force

    def send(j):
        return pltpu.make_async_remote_copy(
            src_ref=forces.at[body],
            dst_ref=forces.at[body],
            send_sem=send_sems.at[j],
            recv_sem=recv_sems.at[body],
            device_id=place(j),
            device_id_type=MESH,
        )

    @pl.when(half == 0)
    def _():
        pl.semaphore_wait(barrier, 2 * (bodies - 1))
        pl.semaphore_signal(go_sem, inc=1, device_id={"col": partner}, device_id_type=MESH)

    @pl.when(half == 1)
    def _():
        pl.semaphore_wait(go_sem, 1)

    each(lambda j: send(j).start())

    loads[0].wait()

    lane = lax.broadcasted_iota(jnp.int32, source.shape[1:], 1)
    spread = []
    for a in range(3):
        rows = jnp.pad(positions[a], ((0, 0), (0, wide - blobs)))
        spread.append(triple(rows, blobs))
        source[a] = spread[a]
        for t in range(2):
            own_rows[3 * t + a : 3 * t + a + 1, :blobs] = positions[a, pl.ds(2 * body + t, 1), :]
    source[3] = jnp.where(
        lane < blobs, spread[0], jnp.where(lane < 2 * blobs, spread[1], spread[2])
    )
    own_cols = own_rows[...].T
    lane = lax.broadcasted_iota(jnp.int32, (pad, wide), 1)
    for t in range(2):
        cols = [
            jnp.broadcast_to(own_cols[:pad, 3 * t + a : 3 * t + a + 1], (pad, wide))
            for a in range(3)
        ]
        for a in range(3):
            own[t, a] = cols[a]
        own[t, 3] = jnp.where(lane < blobs, cols[0], jnp.where(lane < 2 * blobs, cols[1], cols[2]))

    lax.fori_loop(0, 2 * bodies, build, 0)

    def product(j):
        return lax.dot_general(
            forces[j],
            tiles[j].reshape(6 * pad, wide),
            (((1,), (1,)), ((), ())),
            preferred_element_type=jnp.float32,
        )

    def receive(j):
        @pl.when(j != body)
        def _():
            pltpu.make_async_remote_copy(
                src_ref=forces.at[j],
                dst_ref=forces.at[j],
                send_sem=send_sems.at[0],
                recv_sem=recv_sems.at[j],
                device_id={"col": partner},
                device_id_type=MESH,
            ).wait_recv()

    group = math.gcd(bodies, GROUP)

    def gather(turn, total):
        picks = [far(bodies - 1 - (turn * group + k)) for k in range(group)]
        for j in picks:
            receive(j)
        for j in picks:
            total = total + product(j)
        return total

    total = jnp.zeros((slip.shape[0], 6 * pad), jnp.float32)
    if bodies <= 8:
        for turn in range(bodies // group):
            total = gather(turn, total)
    else:
        total = lax.fori_loop(0, bodies // group, gather, total)
    full = round_up(6 * pad, LANES)
    total = jnp.pad(total, ((0, 0), (0, full - 6 * pad)))
    lane = lax.broadcasted_iota(jnp.int32, total.shape, 1)

    def moved(by):
        return pltpu.roll(total, full - by, 1) if by else total

    for t in range(2):
        start = 3 * t * pad
        shift = pad - blobs
        value = jnp.where(
            lane < blobs,
            moved(start),
            jnp.where(lane < 2 * blobs, moved(start + shift), moved(start + 2 * shift)),
        )
        part[t] = value[:, :wide]
    part_swap = swap(part, other_part, part_sems)
    part_swap.start()

    each(lambda j: send(j).wait_send())
    part_swap.wait()
    mine = slip[...] - (part[half] + other_part[half])[:, :narrow]
    residual[0] = mine
    theirs = other_slip[...] - (part[1 - half] + other_part[1 - half])[:, :narrow]
    result = held[...] + (apply(mine, half) + apply(theirs, 1 - half))
    updated[0] = result[:, :narrow]


def finish(updated, residual, updated_out, residual_out, sems):
    copies = [
        pltpu.make_async_copy(updated, updated_out, sems.at[0]),
        pltpu.make_async_copy(residual, residual_out, sems.at[1]),
    ]
    for copy in copies:
        copy.start()
    for copy in copies:
        copy.wait()


def stay(value):
    return pltpu.with_memory_space_constraint(value, pltpu.HBM)


def local(slip, inverse, positions):
    row_count = lax.axis_size("row")
    col_count = lax.axis_size("col")
    count = row_count * col_count
    bodies = count // 2
    blobs = positions.shape[2]
    rows, narrow = slip.shape[1:]
    wide = round_up(narrow, LANES)
    pad = round_up(blobs, CHUNK)
    vmem = pl.BlockSpec(memory_space=pltpu.VMEM)
    f32, bf16 = jnp.float32, jnp.bfloat16
    dma = pltpu.SemaphoreType.DMA
    tile_bytes = bodies * 6 * pad * wide * 2
    updated, residual = pl.pallas_call(
        functools.partial(kernel, row_count, col_count, blobs),
        out_shape=(
            pltpu.VMEM(slip.shape, f32),
            pltpu.VMEM(slip.shape, f32),
        ),
        in_specs=[pl.BlockSpec(memory_space=pltpu.HBM)] * 3,
        out_specs=(vmem, vmem),
        scratch_shapes=[
            pltpu.VMEM((rows, narrow), f32),
            pltpu.VMEM(inverse.shape[1:], f32),
            pltpu.VMEM((3, count, blobs), f32),
            pltpu.VMEM((2, wide, wide), bf16),
            pltpu.VMEM((2, wide, wide), bf16),
            pltpu.VMEM((bodies, 2, 3 * pad, wide), bf16),
            pltpu.VMEM((8, LANES), f32),
            pltpu.VMEM((2, 4, pad, wide), f32),
            pltpu.VMEM((4, count, wide), f32),
            pltpu.VMEM((rows, narrow), f32),
            pltpu.VMEM((2, rows, wide), f32),
            pltpu.VMEM((2, rows, wide), f32),
            pltpu.VMEM((bodies, rows, wide), bf16),
            pltpu.VMEM((rows, wide), f32),
            dma((3,)),
            dma((2,)),
            dma((2,)),
            dma((bodies,)),
            dma((bodies,)),
            pltpu.SemaphoreType.REGULAR,
        ],
        compiler_params=pltpu.CompilerParams(
            collective_id=0,
            has_side_effects=True,
            vmem_limit_bytes=2 * tile_bytes if 2 * tile_bytes < 2**24 else 60 * 2**20,
        ),
    )(*(stay(v) for v in (slip, jnp.swapaxes(inverse, 0, 1), jnp.swapaxes(positions, 0, 1))))
    return pl.pallas_call(
        finish,
        out_shape=(jax.ShapeDtypeStruct(slip.shape, f32),) * 2,
        in_specs=[vmem, vmem],
        out_specs=(pl.BlockSpec(memory_space=pltpu.HBM),) * 2,
        scratch_shapes=[dma((2,))],
        compiler_params=pltpu.CompilerParams(vmem_limit_bytes=2**20),
    )(updated, residual)


def solution(mesh):
    in_specs = (
        P(("groups", "row", "col"), None, None),
        P(("groups", "row", "col"), None, None),
        P("groups", None, None),
    )
    out_specs = (P(("groups", "row", "col"), None, None), P(("groups", "row", "col"), None, None))
    return jax.shard_map(local, mesh=mesh, in_specs=in_specs, out_specs=out_specs, check_vma=False)
```
